256 devices in a mesh: dp: 64 (over y, z, core), tensor: 4 (over x).
Axes of the slice: x: 4, y: 4, z: 8, core: 2. Of those that a mesh axis runs over, the one named last changes fastest.
Arguments:
- hidden: bfloat16 [1024, 4096], P(('dp', 'tensor')), may hold values from -6 to 6
- shortcut: bfloat16 [1024, 4096], P('dp'), may hold values from -6 to 6
- expert_ids: int32 [1024, 2], P('dp'), may hold values from 0 to 7, all different within a row; in each aligned block of 16 rows (0 to 15, 16 to 31, ...) at most 6 rows name the same one
- route_weight: float32 [1024, 2], P('dp'), may hold values from 0.1 to 1
- dense_gain: float32 [4096], replicated, may hold values from 0.5 to 1.5
- moe_gain: float32 [4096], replicated, may hold values from 0.5 to 1.5
- dense_gate: bfloat16 [4096, 8192], P(None, 'dp'), may hold values from -0.09375 to 0.09375
- dense_lift: bfloat16 [4096, 8192], P(None, 'dp'), may hold values from -0.09375 to 0.09375
- dense_down: bfloat16 [8192, 4096], P('dp'), may hold values from -0.0625 to 0.0625
- expert_gate: bfloat16 [4096, 65536], P(None, ('dp', 'tensor')), may hold values from -0.09375 to 0.09375
- expert_lift: bfloat16 [4096, 65536], P(None, ('dp', 'tensor')), may hold values from -0.09375 to 0.09375
- expert_down: bfloat16 [65536, 4096], P(('dp', 'tensor')), may hold values from -0.0625 to 0.0625
Outputs:
- mixed: bfloat16 [1024, 4096], P(('dp', 'tensor'))
The draws below stay inside these ranges and needn't reach their ends.
Inputs may be any that keep to these rules, and one draw needn't show every extreme that they name: `expert_ids`: the 2 experts of a token differ. In each aligned block of 16 rows (the tokens of one index of dp) no expert is named by more than 6 rows, and in every draw some expert is named by exactly 6 rows of some block; every expert is named somewhere.
All inputs are finite; a program needn't handle non-finite values.
Results may differ from the reference program's by a relative error of at most 0.006.
Values may be sent and summed in bfloat16 or wider, within the bound.
No kernel may reach another device: no remote copies, remote signals or barrier semaphores. Data moves between devices by JAX's collectives and lax.ppermute only.
A program may use at most 64 MiB of HBM per device.

```python
import math
import jax
import jax.numpy as jnp
import numpy as np
from jax import lax

D = 4096
E = 8
TOP = 2
FF = 8192
FF_E = 8192
TOK_DEV = 16
CAP = 6
SLICE = 256
TOKENS = 1024


def shard_levels(key, extent, split, smallest, largest):
    def one(axis_at, blocks):
        heights = jax.random.uniform(jax.random.fold_in(jax.random.fold_in(key, 6), axis_at), (blocks,), jnp.float32, smallest / len(split), largest / len(split))
        return jnp.repeat(jnp.exp(heights), extent[axis_at] // blocks).reshape((-1,) + (1,) * (len(extent) - axis_at - 1))

    level = one(*split[0])
    for cut in split[1:]:
        level = level * one(*cut)
    return level


def deal_out(key, own, number, rows, amount, top, limit, lean):
    sequence = jax.random.permutation(key, amount)
    packed, usual = portions_of(amount, rows * top, limit, lean, True), portions_of(amount, rows * top, limit, lean, False)
    places = jnp.arange(amount)

    def named(lengths, offset_by):
        used = int((lengths > 0).sum())
        fixed = max(1, used // 4)
        shifted = fixed + (places - fixed + offset_by * (used - fixed)) % max(1, amount - fixed)
        return jnp.zeros((amount,), jnp.int32).at[sequence[jnp.where(places < fixed, places, shifted)]].set(jnp.asarray(lengths, jnp.int32))

    lengths = jnp.where(number % 4 == 0, named(packed, number // 4), named(usual, number - number // 4 - 1))
    mixed = jax.random.permutation(jax.random.fold_in(own, 3), amount)
    giver, sink = mixed[0:amount // 2 * 2:2], mixed[1:amount // 2 * 2:2]
    margin = jnp.minimum(lengths[giver] - 1, limit - lengths[sink]) // 2
    margin = jnp.where((giver == sequence[0]) | (sink == sequence[0]) | (lengths[sink] == 0), 0, jnp.maximum(margin, 0))
    shifted = jax.random.randint(jax.random.fold_in(own, 4), (amount // 2,), 0, 1 << 20) % (margin + 1)
    lengths = lengths.at[giver].add(-shifted).at[sink].add(shifted)
    items = jnp.searchsorted(jnp.cumsum(lengths), jnp.arange(rows * top), side="right").astype(jnp.int32)
    grid = items.reshape(top, rows).T
    grid = grid[jax.random.permutation(jax.random.fold_in(own, 1), rows)]
    offset_by = jax.random.randint(jax.random.fold_in(own, 2), (rows, 1), 0, top)
    return jnp.take_along_axis(grid, (jnp.arange(top)[None, :] + offset_by) % top, axis=1)


def portions_of(number_of, total, most, slope, full):
    weights = [(1 << 20) // math.isqrt(grade ** slope) + 1 for grade in range(1, number_of + 1)]
    largest = most if full else min(most, max(-(-total // number_of), total * weights[0] // sum(weights)))
    least = 1 if total - largest >= number_of - 1 else 0
    counts, surplus = [largest] + [least] * (number_of - 1), total - largest - least * (number_of - 1)
    while surplus > 0:
        movable = [i for i in range(1, number_of) if counts[i] < largest] or [i for i in range(1, number_of) if counts[i] < most]
        pool, remaining = sum([weights[i] for i in movable]), surplus
        for i in movable:
            extra = min(most - counts[i], max(1, remaining * weights[i] // pool), surplus)
            counts[i] = counts[i] + extra
            surplus = surplus - extra
    return np.array(counts)


def scatter_about(own_key, extent, scale, limit, split=(), kind=jnp.bfloat16):
    array = jax.random.normal(own_key, extent, jnp.float32) * scale
    if len(split) > 0:
        array = shard_levels(own_key, extent, split, -0.22, 0.18) * array
    return jnp.clip(array, min=-limit, max=limit).astype(kind)


def setup_inputs(seed: int = 0) -> dict:
    splits = jax.random.split(jax.random.key(seed), 13)
    hidden = scatter_about(splits[0], (TOKENS, D), 1.0, 6.0, ((0, 256),))
    shortcut = scatter_about(splits[1], (TOKENS, D), 1.0, 6.0, ((0, 64),))
    expert_ids_keys = jax.random.split(jax.random.fold_in(splits[2], 1), TOKENS // TOK_DEV)
    expert_ids_turns = jax.random.permutation(jax.random.fold_in(splits[2], 3), TOKENS // TOK_DEV)
    expert_ids = jax.vmap(lambda own, number: deal_out(jax.random.fold_in(splits[2], 2), own, number, TOK_DEV, E, TOP, CAP, 2))(expert_ids_keys, expert_ids_turns).reshape((TOKENS, TOP))
    route_weight = jnp.clip(0.1 + 0.9 * jax.random.uniform(splits[3], (TOKENS, TOP), jnp.float32) ** shard_levels(splits[3], (TOKENS, TOP), ((0, 64),), -0.2, 0.2), 0.1, 1.0)
    dense_gain = jnp.clip(jax.random.uniform(splits[4], (D,), jnp.float32, 0.5, 1.5), 0.5, 1.5)
    moe_gain = jnp.clip(jax.random.uniform(splits[5], (D,), jnp.float32, 0.5, 1.5), 0.5, 1.5)
    dense_gate = scatter_about(splits[6], (D, FF), D ** -0.5, 0.09375, ((1, 64),))
    dense_lift = scatter_about(splits[7], (D, FF), D ** -0.5, 0.09375, ((1, 64),))
    dense_down = scatter_about(splits[8], (FF, D), FF ** -0.5, 0.0625, ((0, 64),))
    expert_gate = scatter_about(splits[9], (D, E * FF_E), D ** -0.5, 0.09375, ((1, 256),))
    expert_lift = scatter_about(splits[10], (D, E * FF_E), D ** -0.5, 0.09375, ((1, 256),))
    expert_down = scatter_about(splits[11], (E * FF_E, D), FF_E ** -0.5, 0.0625, ((0, 256),))
    return {"hidden": hidden, "shortcut": shortcut, "expert_ids": expert_ids, "route_weight": route_weight, "dense_gain": dense_gain, "moe_gain": moe_gain, "dense_gate": dense_gate, "dense_lift": dense_lift, "dense_down": dense_down, "expert_gate": expert_gate, "expert_lift": expert_lift, "expert_down": expert_down}


EPSILON = 1e-05

def normalize(values_in, gain):
    values = values_in.astype(jnp.float32)
    scale = lax.rsqrt(lax.optimization_barrier(jnp.mean(values * values, axis=-1, keepdims=True)) + EPSILON)
    return (values * scale * gain).astype(jnp.bfloat16)

def slot_places(expert_ids):
    blocks = expert_ids.shape[0] // TOK_DEV
    flat = expert_ids.reshape(blocks, TOK_DEV * TOP)
    picked = (flat[:, :, None] == jnp.arange(E, dtype=jnp.int32)[None, None, :]).astype(jnp.int32)
    before = jnp.cumsum(picked, axis=1) - picked
    ranks = lax.optimization_barrier(jnp.sum(before * picked, axis=2))
    return flat * CAP + ranks

def reference(hidden, shortcut, expert_ids, route_weight, dense_gain, moe_gain, dense_gate, dense_lift, dense_down, expert_gate, expert_lift, expert_down):
    normed = normalize(hidden, dense_gain)
    gate_vals = jnp.dot(normed, dense_gate, preferred_element_type=jnp.float32)
    lift_vals = jnp.dot(normed, dense_lift, preferred_element_type=jnp.float32)
    dense_inner = (jax.nn.silu(gate_vals) * lift_vals).astype(jnp.bfloat16)
    dense_out = jnp.dot(dense_inner, dense_down, preferred_element_type=jnp.float32)
    moe_in = normalize(shortcut, moe_gain)
    blocks = TOKENS // TOK_DEV
    places = slot_places(expert_ids)
    chosen = (places[:, :, None] == jnp.arange(E * CAP, dtype=jnp.int32)[None, None, :]).astype(jnp.float32)
    chosen = chosen.reshape(blocks, TOK_DEV, TOP, E * CAP)
    spread = lax.optimization_barrier(jnp.sum(chosen, axis=2))
    weighted = lax.optimization_barrier(jnp.sum(chosen * route_weight.reshape(blocks, TOK_DEV, TOP, 1), axis=2))
    grouped = moe_in.astype(jnp.float32).reshape(blocks, TOK_DEV, D)
    buffer = jnp.einsum('bts,btd->bsd', spread, grouped).astype(jnp.bfloat16).reshape(blocks, E, CAP, D)
    parts = FF_E // SLICE

    def one_expert(expert):
        rows_in = lax.dynamic_index_in_dim(buffer, expert, 1, keepdims=False).reshape(blocks * CAP, D)
        start = expert * FF_E
        gate_part = jnp.dot(rows_in, lax.dynamic_slice_in_dim(expert_gate, start, FF_E, 1), preferred_element_type=jnp.float32)
        lift_part = jnp.dot(rows_in, lax.dynamic_slice_in_dim(expert_lift, start, FF_E, 1), preferred_element_type=jnp.float32)
        inner = (jax.nn.silu(gate_part) * lift_part).astype(jnp.bfloat16)

        def add_part(total, index):
            first = index * SLICE
            term = jnp.dot(lax.dynamic_slice_in_dim(inner, first, SLICE, 1), lax.dynamic_slice_in_dim(expert_down, start + first, SLICE, 0), preferred_element_type=jnp.float32).astype(jnp.bfloat16)
            term = lax.optimization_barrier(term)
            return (total + term.astype(jnp.float32), None)
        return lax.scan(add_part, jnp.zeros((blocks * CAP, D), jnp.float32), jnp.arange(parts, dtype=jnp.int32))[0]
    outputs = lax.map(one_expert, jnp.arange(E, dtype=jnp.int32))
    outputs = outputs.reshape(E, blocks, CAP, D).transpose(1, 0, 2, 3).reshape(blocks, E * CAP, D)
    moe_out = jnp.einsum('bts,bsd->btd', weighted, outputs, precision=lax.Precision.HIGHEST).reshape(TOKENS, D)
    return (hidden.astype(jnp.float32) + dense_out + moe_out).astype(jnp.bfloat16)
```

```python
import functools

import jax
import jax.numpy as jnp
from jax import lax
from jax.experimental import pallas as pl
from jax.experimental.pallas import tpu as pltpu
from jax.sharding import Mesh, PartitionSpec as P

D = 4096
E = 8
TOP = 2
CAP = 6
EPSILON = 1e-05


BF16 = jnp.bfloat16
F32 = jnp.float32
VMEM = pl.BlockSpec(memory_space=pltpu.VMEM)


def to_all(block, axis):
    n = lax.axis_size(axis)
    return lax.all_to_all(jnp.broadcast_to(block[None], (n, *block.shape)), axis, 0, 0, tiled=True)


def exchanged(blocks, axis):
    return lax.all_to_all(blocks, axis, 0, 0, tiled=True)


def summed(blocks):
    return jnp.sum(blocks.astype(F32), axis=0)


def swap(value, axis, k):
    n = lax.axis_size(axis)
    return lax.ppermute(value, axis, [(i, i ^ k) for i in range(n)])


def call(kernel, inputs, outputs, scratch=(), flops=0):
    shapes = [jax.ShapeDtypeStruct(shape, dtype) for shape, dtype in outputs]
    sizes = [x.size * x.dtype.itemsize for x in (*inputs, *shapes)]
    sizes += [x.size * jnp.dtype(x.dtype).itemsize for x in map(lambda s: jax.ShapeDtypeStruct(*s), scratch)]
    return pl.pallas_call(
        kernel,
        out_shape=shapes,
        in_specs=[VMEM] * len(inputs),
        out_specs=[VMEM] * len(shapes),
        scratch_shapes=[pltpu.VMEM(shape, dtype) for shape, dtype in scratch],
        cost_estimate=pl.CostEstimate(flops=flops, bytes_accessed=sum(sizes), transcendentals=0),
        compiler_params=pltpu.CompilerParams(vmem_limit_bytes=sum(sizes) + (6 << 20)),
    )(*inputs)


def gated(x, gate, lift):
    gate_vals = dot(x, gate)
    return (gate_vals / (1.0 + jnp.exp(-gate_vals)) * dot(x, lift)).astype(BF16)


def expert_inner(x_ref, gate_ref, lift_ref):
    blocks, _, width = x_ref.shape
    gate_vals = lift_vals = 0.0
    for k in range(blocks):
        x = x_ref[k]
        gate_vals += dot(x, gate_ref[k * width : (k + 1) * width, :])
        lift_vals += dot(x, lift_ref[k * width : (k + 1) * width, :])
    return (gate_vals / (1.0 + jnp.exp(-gate_vals)) * lift_vals).astype(BF16)


def inner_kernel(x_ref, gate_ref, lift_ref, inner_ref):
    inner_ref[...] = expert_inner(x_ref, gate_ref, lift_ref)


def terms_kernel(x_ref, gate_ref, lift_ref, down_ref, terms_ref):
    inner = expert_inner(x_ref, gate_ref, lift_ref)
    blocks, _, width = terms_ref.shape
    for k in range(blocks):
        terms_ref[k] = dot(inner, down_ref[:, k * width : (k + 1) * width]).astype(BF16)


def add_terms_kernel(inner_ref, down_ref, back_ref, terms_ref):
    blocks, _, width = terms_ref.shape
    for k in range(blocks):
        total = dot(inner_ref[...], down_ref[:, k * width : (k + 1) * width]) + back_ref[k].astype(F32)
        terms_ref[k] = total.astype(BF16)


def dense_kernel(count, *refs):
    pieces, (gate_ref, lift_ref, down_ref, own_ref, other_ref, x_ref) = refs[:count], refs[count:]
    at = 0
    for piece in pieces:
        x_ref[at : at + piece.shape[0], :] = piece[...]
        at += piece.shape[0]
    inner = gated(x_ref[...], gate_ref[...], lift_ref[...])
    half = own_ref.shape[0]
    for k in range(0, D, 1024):
        own_ref[:, k : k + 1024] = dot(inner[:half], down_ref[:, k : k + 1024])
        other_ref[:, k : k + 1024] = dot(inner[half:], down_ref[:, k : k + 1024]).astype(BF16)


def scale_of(values):
    return lax.rsqrt(jnp.mean(values * values, axis=-1, keepdims=True) + EPSILON)


def dot(a, b):
    return jnp.dot(a, b, preferred_element_type=F32)


def local(
    hidden,
    shortcut,
    expert_ids,
    route_weight,
    dense_gain,
    moe_gain,
    dense_gate,
    dense_lift,
    dense_down,
    expert_gate,
    expert_lift,
    expert_down,
):
    t = lax.axis_index("t")
    tokens = shortcut.shape[0]
    width = D // 4

    flat = expert_ids.reshape(tokens * TOP)
    picked = (flat[:, None] == jnp.arange(E, dtype=jnp.int32)[None, :]).astype(jnp.int32)
    before = jnp.cumsum(picked, axis=0) - picked
    places = flat * CAP + jnp.sum(before * picked, axis=1)
    chosen = (places[:, None] == jnp.arange(E * CAP, dtype=jnp.int32)[None, :]).astype(F32)
    chosen = chosen.reshape(tokens, TOP, E * CAP)
    spread = jnp.sum(chosen, axis=1).astype(BF16)
    weighted = jnp.sum(chosen * route_weight[:, :, None], axis=1)

    scale = scale_of(shortcut.astype(F32))
    part = lax.dynamic_slice_in_dim(shortcut, t * width, width, 1).astype(F32)
    gain = lax.dynamic_slice_in_dim(moe_gain, t * width, width, 0)
    moe_in = (part * scale * gain).astype(BF16)
    buffer = lax.dot_general(spread, moe_in, (((0,), (0,)), ((), ())), preferred_element_type=F32)
    buffer = buffer.astype(BF16).reshape(E, CAP, width)

    hidden32 = hidden.astype(F32)
    normed = (hidden32 * scale_of(hidden32) * dense_gain).astype(BF16)

    outgoing = jnp.repeat(buffer, 4, axis=0)
    rows = exchanged(outgoing, ("y", "z")).reshape(-1, width)
    count = rows.shape[0]
    own = to_all(rows, "t")
    other = swap(own, "c", 1)

    group = normed
    for k in (4, 2, 1):
        group = jnp.concatenate([group, swap(group, "z", k)], axis=0)
    size = group.shape[0]
    near1, near3 = swap(group, "y", 1), swap(group, "y", 3)
    far = [swap(near1[: size // 2], "y", 3), swap(near3[size // 2 :], "y", 1)]
    pieces = [group, near1, *far, near3]
    pieces += [swap(piece, "c", 1) for piece in pieces]

    hidden_units = expert_gate.shape[1]
    products = 2 * count * D * hidden_units
    (inner,) = call(
        inner_kernel, (own, expert_gate, expert_lift), [((count, hidden_units), BF16)], flops=2 * products
    )
    (partner,) = call(
        terms_kernel, (other, expert_gate, expert_lift, expert_down), [(own.shape, BF16)], flops=3 * products
    )
    back = swap(partner, "c", 1)
    (terms,) = call(add_terms_kernel, (inner, expert_down, back), [(own.shape, BF16)], flops=products)
    sums = summed(exchanged(terms, "t")).astype(BF16).reshape(-1, CAP, width)
    returned = exchanged(sums, ("y", "z"))
    expert_out = jnp.sum(returned.astype(F32).reshape(E, 4, CAP, width), axis=1).reshape(E * CAP, width)

    dense_rows = 4 * size
    dense_terms, dense_partner = call(
        functools.partial(dense_kernel, len(pieces)),
        (*pieces, dense_gate, dense_lift, dense_down),
        [((dense_rows, D), F32), ((dense_rows, D), BF16)],
        scratch=[((2 * dense_rows, D), BF16)],
        flops=12 * dense_rows * D * dense_gate.shape[1],
    )
    dense_total = dense_terms + swap(dense_partner, "c", 1).astype(F32)
    block = [dense_total[k * size : (k + 1) * size] for k in range(4)]
    via1 = swap(block[2][: size // 2].astype(BF16), "y", 1).astype(F32)
    via3 = swap(block[2][size // 2 :].astype(BF16), "y", 3).astype(F32)
    to3 = jnp.concatenate([block[3][: size // 2] + via1, block[3][size // 2 :]], axis=0).astype(BF16)
    to1 = jnp.concatenate([block[1][: size // 2], block[1][size // 2 :] + via3], axis=0).astype(BF16)
    total = block[0] + swap(to1, "y", 1).astype(F32) + swap(to3, "y", 3).astype(F32)
    for k in (1, 2, 4):
        size //= 2
        total = total[:size] + swap(total[size:].astype(BF16), "z", k).astype(F32)
    dense_out = total

    moe = jnp.dot(weighted, expert_out, precision=lax.Precision.HIGHEST, preferred_element_type=F32)
    got = exchanged(moe.reshape(4, tokens // 4, width), "t")
    moe_out = jnp.moveaxis(got, 0, 1).reshape(tokens // 4, D)
    return (hidden32 + dense_out + moe_out).astype(BF16)


def solution(mesh):
    fine = Mesh(mesh.devices.reshape(4, 8, 2, 4), ("y", "z", "c", "t"))
    dp = ("y", "z", "c")
    every = ("y", "z", "c", "t")
    in_specs = (
        P(every, None),
        P(dp, None),
        P(dp, None),
        P(dp, None),
        P(),
        P(),
        P(None, dp),
        P(None, dp),
        P(dp, None),
        P(None, every),
        P(None, every),
        P(every, None),
    )
    return jax.shard_map(local, mesh=fine, in_specs=in_specs, out_specs=P(every, None), check_vma=False)
```
